512 devices in a mesh: segment: 4 (over x_lo, core), ctx: 128 (over z, y, x_hi).
Axes of the slice: x: 4 (x_hi: 2, x_lo: 2; x = x_hi * 2 + x_lo), y: 4, z: 16, core: 2. Of those that a mesh axis runs over, the one named last changes fastest.
Arguments:
- queries: bfloat16 [4, 26624, 4096], P('segment', 'ctx'), may hold values from -8 to 8
- key_value_heads: bfloat16 [4, 26624, 1024], P('segment', 'ctx'), may hold values from -8 to 8
- doc_lengths: int32 [4, 64], P('segment'), may hold values from 1 to 1664, 26624 in all within a row
- norm_gain: float32 [4, 4096], P('segment'), may hold values from 0.5 to 1.5
Outputs:
- handed: bfloat16 [4, 26624, 4096], P('segment', 'ctx')
The draws below stay inside these ranges and needn't reach their ends.
Inputs may be any that keep to these rules, and one draw needn't show every extreme that they name: `doc_lengths`: each row sums to 26624; its largest entry is 1664.
All inputs are finite; a program needn't handle non-finite values.
Results may differ from the reference program's by a relative error of at most 0.012.
The reference program's roundings to bfloat16 on the way count: a program that leaves them out, or rounds other values in their place, can miss the bound.
Values may be sent and summed in bfloat16 or wider, within the bound.
A program may use at most 64 MiB of HBM per device.

```python
import math
import jax
import jax.numpy as jnp
import numpy as np
from jax import lax

QUERY_HEADS = 32
KEY_VALUE_HEADS = 4
HEAD_SIZE = 128
TOK_DEV = 208
RELAY_SECTIONS = 4
PACKED_TOKENS = 26624
SPAN = 8
DOC_MOST = 1664
NDOC = 64
N_CTX = 128


def draw_queries(key, part):
    array_shape = (RELAY_SECTIONS, PACKED_TOKENS, QUERY_HEADS * HEAD_SIZE)
    base_key = jax.random.fold_in(key, 1)
    base_offset = jnp.clip(jax.random.normal(base_key, array_shape, jnp.float32), -4.0, 4.0)
    return base_offset.astype(jnp.bfloat16)


def draw_key_value_heads(key, part):
    array_shape = (RELAY_SECTIONS, PACKED_TOKENS, 2 * KEY_VALUE_HEADS * HEAD_SIZE)
    base_key = jax.random.fold_in(key, 2)
    base_offset = jnp.clip(jax.random.normal(base_key, array_shape, jnp.float32), -4.0, 4.0)
    return base_offset.astype(jnp.bfloat16)


def split_up(amount, total, most, slope):
    loads = [(1 << 20) // math.isqrt(standing ** slope) + 1 for standing in range(2, amount + 1)]
    surplus, counts = total - most - (amount - 1), [1] * (amount - 1)
    while surplus > 0:
        free = [i for i in range(amount - 1) if counts[i] < most]
        whole, left = sum([loads[i] for i in free]), surplus
        for i in free:
            more = min(most - counts[i], max(1, left * loads[i] // whole), surplus)
            counts[i] = counts[i] + more
            surplus = surplus - more
    return np.array([most] + counts)


def ragged(key, number_of, total, bound, slope):
    if number_of == 2:
        one = jax.random.randint(key, (), max(1, total - bound), min(bound, total - 1) + 1)
        return jnp.stack([one, total - one])
    tallies = jnp.asarray(split_up(number_of, total, bound, slope), jnp.int32)
    couples = (number_of - 1) // 2
    giver, taker = tallies[1:1 + 2 * couples:2], tallies[2:2 + 2 * couples:2]
    room = jnp.minimum(giver - 1, bound - taker)
    moved = jax.random.randint(jax.random.fold_in(key, 1), (couples,), 0, 1 << 20) % (room + 1)
    tallies = tallies.at[1:1 + 2 * couples:2].set(giver - moved).at[2:2 + 2 * couples:2].set(taker + moved)
    return tallies[jax.random.permutation(jax.random.fold_in(key, 2), number_of)]


def setup_inputs(seed: int = 0) -> dict:
    streams_of = jax.random.split(jax.random.key(seed), 5)
    queries = draw_queries(jax.random.fold_in(streams_of[4], 71), 0)
    key_value_heads = draw_key_value_heads(jax.random.fold_in(streams_of[4], 71), 0)
    doc_lengths = jax.vmap(lambda own: ragged(own, NDOC, PACKED_TOKENS, DOC_MOST, 2))(jax.random.split(streams_of[2], RELAY_SECTIONS)).reshape((RELAY_SECTIONS, NDOC)).astype(jnp.int32)
    norm_gain = jnp.clip(1.0 + 0.1 * jax.random.normal(streams_of[3], (RELAY_SECTIONS, QUERY_HEADS * HEAD_SIZE), jnp.float32), 0.5, 1.5)
    return {"queries": queries, "key_value_heads": key_value_heads, "doc_lengths": doc_lengths, "norm_gain": norm_gain}


def sign_table(size):
    rows = lax.broadcasted_iota(jnp.int32, (size, size), 0)
    cols = lax.broadcasted_iota(jnp.int32, (size, size), 1)
    parity = jnp.zeros((size, size), jnp.int32)
    for level in range(size.bit_length() - 1):
        parity = parity + rows // 2 ** level % 2 * (cols // 2 ** level % 2)
    return jnp.where(parity % 2 == 0, 1.0, -1.0).astype(jnp.float32)

def hadamard_rotate_heads(values, heads, lookup_table):
    token_rows = values.shape[0]
    width = lookup_table.shape[0]
    split = values.astype(jnp.float32).reshape(token_rows, heads, width)
    turned = jnp.einsum('thd,de->the', split, lookup_table, precision=lax.Precision.HIGHEST)
    return (turned * width ** (-0.5)).astype(jnp.bfloat16)

def doc_index(starts, positions):
    return lax.optimization_barrier(jnp.sum((starts[None, :] <= positions[:, None]).astype(jnp.int32), axis=1, dtype=jnp.int32)) - 1

def reference(queries, key_value_heads, doc_lengths, norm_gain):
    lookup_table = sign_table(HEAD_SIZE)
    query_group = QUERY_HEADS // KEY_VALUE_HEADS
    scale = HEAD_SIZE ** (-0.5)
    window = (SPAN + 1) * TOK_DEV
    pad_margin = SPAN * TOK_DEV
    results = []
    for relay_segment in range(RELAY_SECTIONS):
        rotated_query = hadamard_rotate_heads(queries[relay_segment], QUERY_HEADS, lookup_table).reshape(PACKED_TOKENS, KEY_VALUE_HEADS, query_group, HEAD_SIZE)
        rotated_key_value = hadamard_rotate_heads(key_value_heads[relay_segment], 2 * KEY_VALUE_HEADS, lookup_table)
        lengths = doc_lengths[relay_segment]
        starts = jnp.cumsum(lengths, dtype=jnp.int32) - lengths
        positions = jnp.arange(PACKED_TOKENS, dtype=jnp.int32)
        docs = doc_index(starts, positions)
        padded_key_value = jnp.concatenate([jnp.zeros((pad_margin, 2 * KEY_VALUE_HEADS, HEAD_SIZE), jnp.bfloat16), rotated_key_value], axis=0)
        padded_pos = jnp.arange(-pad_margin, PACKED_TOKENS, dtype=jnp.int32)
        padded_doc = doc_index(starts, padded_pos)

        def one_block(index):
            begin = (index * TOK_DEV).astype(jnp.int32)
            q_blk = lax.dynamic_slice_in_dim(rotated_query, begin, TOK_DEV, 0)
            q_pos = lax.dynamic_slice_in_dim(positions, begin, TOK_DEV, 0)
            q_doc = lax.dynamic_slice_in_dim(docs, begin, TOK_DEV, 0)
            key_value_block = lax.dynamic_slice_in_dim(padded_key_value, begin, window, 0)
            k_pos = lax.dynamic_slice_in_dim(padded_pos, begin, window, 0)
            k_doc = lax.dynamic_slice_in_dim(padded_doc, begin, window, 0)
            allowed = (k_pos[None, :] <= q_pos[:, None]) & (k_doc[None, :] == q_doc[:, None])
            mask = allowed[None, :, None, :]
            key_rows = key_value_block[:, :KEY_VALUE_HEADS].astype(jnp.float32)
            value_rows = key_value_block[:, KEY_VALUE_HEADS:].astype(jnp.float32)
            scores = jnp.einsum('thgd,shd->htgs', q_blk.astype(jnp.float32), key_rows, precision=lax.Precision.HIGHEST) * scale
            scores = jnp.where(mask, scores, -jnp.inf)
            top = lax.optimization_barrier(jnp.max(scores, axis=-1))
            weights = jnp.where(mask, jnp.exp(scores - top[..., None]), 0.0)
            total = lax.optimization_barrier(jnp.sum(weights, axis=-1))
            rounded = lax.optimization_barrier(weights.astype(jnp.bfloat16)).astype(jnp.float32)
            mixed = jnp.einsum('htgs,shd->htgd', rounded, value_rows, precision=lax.Precision.HIGHEST)
            heads_out = mixed / total[..., None]
            restored = jnp.einsum('htgd,de->thge', heads_out, lookup_table, precision=lax.Precision.HIGHEST) * scale
            return restored.reshape(TOK_DEV, QUERY_HEADS * HEAD_SIZE).astype(jnp.bfloat16)
        blocks = lax.map(one_block, jnp.arange(N_CTX, dtype=jnp.int32))
        results.append(blocks.reshape(PACKED_TOKENS, QUERY_HEADS * HEAD_SIZE))
    outputs = []
    for relay_segment in range(RELAY_SECTIONS):
        source = lax.optimization_barrier(results[(relay_segment - 1) % RELAY_SECTIONS]).astype(jnp.float32)
        power = lax.optimization_barrier(jnp.mean(source * source, axis=-1, keepdims=True))
        normed = source * lax.rsqrt(power + 1e-05) * norm_gain[relay_segment][None, :]
        outputs.append(normed.astype(jnp.bfloat16))
    return jnp.stack(outputs, axis=0)
```

```python
import functools

import jax
import jax.numpy as jnp
import numpy as np
from jax import lax
from jax.experimental import pallas as pl
from jax.experimental.pallas import tpu as pltpu
from jax.sharding import PartitionSpec as P

QUERY_HEADS = 32
KEY_VALUE_HEADS = 4
HEAD = 128
GROUP = QUERY_HEADS // KEY_VALUE_HEADS
NDOC = 64
SPAN = 8
SLOTS = SPAN + 3
MESH = pl.DeviceIdType.MESH
PV, ZO, ZP, D2O, D2P, D4O, D4P, D6O, D6P, RELAY = range(10)
SENDS = 10
CHUNK = 256
LOW = -1e30


def hadamard(size):
    rows = lax.broadcasted_iota(jnp.int32, (size, size), 0)
    cols = lax.broadcasted_iota(jnp.int32, (size, size), 1)
    both = rows & cols
    both = both ^ (both >> 4)
    both = both ^ (both >> 2)
    both = both ^ (both >> 1)
    return jnp.where((both & 1) == 0, 1.0, -1.0).astype(jnp.bfloat16)


def interleave(*parts):
    parts = list(parts)
    while parts:
        for part in list(parts):
            try:
                next(part)
            except StopIteration:
                parts.remove(part)


def kernel(
    tok, planes, sections,
    q_hbm, kv_ref, len_ref, gain_ref, out_ref,
    q_ref, kvb, qr, scores, tops, tri, att, got, lens,
    q_sem, send_sem, recv_sem, att_send, att_recv,
):
    width = -(-((SPAN + 1) * tok) // 128) * 128
    scale = HEAD ** (-0.5)
    c = lax.axis_index("ctx")
    s = lax.axis_index("segment")
    h = lax.rem(c, 2)
    y = lax.rem(c // 2, 4)
    z = c // 8
    e = 1 - 2 * h
    up = lax.rem(z + 1, planes)
    down = lax.rem(z + planes - 1, planes)
    right = lax.rem(y + 1, 4)
    left = lax.rem(y + 3, 4)

    def at(zz, yy, hh):
        return zz * 8 + yy * 2 + hh

    partner = {"ctx": at(z, y, 1 - h)}
    above = {"ctx": at(up, y, h)}
    below = {"ctx": at(down, y, h)}
    to_right = {"ctx": at(z, right, h)}
    to_left = {"ctx": at(z, left, h)}
    after = {"segment": lax.rem(s + 1, sections)}
    before = {"segment": lax.rem(s + sections - 1, sections)}

    q_copy = pltpu.make_async_copy(q_hbm, q_ref, q_sem)
    q_copy.start()
    barrier = pltpu.get_barrier_semaphore()
    for who in (partner, below, above, to_right, to_left, before, after):
        pl.semaphore_signal(barrier, inc=1, device_id=who, device_id_type=MESH)

    had = hadamard(HEAD)

    def turn(x):
        return (jnp.dot(x, had, preferred_element_type=jnp.float32) * scale).astype(jnp.bfloat16)

    def rows(slot):
        return pl.ds(pl.multiple_of(slot * tok, 16), tok)

    def send(g, k, src, dst, role, who):
        return pltpu.make_async_remote_copy(
            src_ref=kvb.at[g, rows(src), :],
            dst_ref=kvb.at[g, rows(dst), :],
            send_sem=send_sem.at[g, k],
            recv_sem=recv_sem.at[g, role],
            device_id=who,
            device_id_type=MESH,
        )

    def arrived(g, role):
        pltpu.make_async_remote_copy(
            src_ref=kvb.at[g, rows(0), :],
            dst_ref=kvb.at[g, rows(0), :],
            send_sem=send_sem.at[g, 0],
            recv_sem=recv_sem.at[g, role],
            device_id=partner,
            device_id_type=MESH,
        ).wait_recv()

    pv = SPAN + e
    pp = lax.rem(e + 10, 10)

    def table(g, yy):
        entries = {None: [], PV: [], ZO: [], ZP: [], D2O: [], D2P: [], D6O: [], D6P: [], RELAY: []}
        count = [3]

        def add(when, src, dst, role, who):
            entries[when].append(functools.partial(send, g, count[0], src, dst, role, who))
            count[0] += 1

        v_dirs = {0: (1, 3), 1: (1,), 2: (1,), 3: ()}[yy]
        p_dirs = {0: (), 1: (-1,), 2: (-1,), 3: (-3, -1)}[yy]
        for d in v_dirs:
            who = to_right if d == 1 else to_left
            own, pair = (D6O, D6P) if d == 1 else (D2O, D2P)
            add(None, SPAN, SPAN - 2 * d, own, who)
            add(PV, pv, SPAN - 2 * d + e, pair, who)
        for d in p_dirs:
            who = to_right if d == -3 else to_left
            own, pair = (D6O, D6P) if d == -3 else (D2O, D2P)
            add(ZO, 0, -2 * d, own, who)
            add(ZP, pp, -2 * d + e, pair, who)
        if yy == 0:
            add(D6O, 6, 4, D4O, to_right)
            add(D2O, 2, 10, RELAY, below)
            add(RELAY, 10, 4, D4O, to_left)
        if yy == 1:
            add(D6O, 6, 4, D4O, to_right)
            add(D2P, 2 + e, 4 + e, D4P, to_left)
        if yy == 2:
            add(D6P, 6 + e, 4 + e, D4P, to_right)
            add(D2P, 2 + e, 4 + e, D4P, to_left)
        if yy == 3:
            add(D2P, 2 + e, 4 + e, D4P, to_left)
            add(D6O, 6, 10, RELAY, above)
            add(RELAY, 10, 4, D4O, to_right)
        return entries

    def common(g):
        return (
            functools.partial(send, g, 0, SPAN, SPAN - e, PV, partner),
            functools.partial(send, g, 1, SPAN, 0, ZO, above),
            functools.partial(send, g, 2, pv, pp, ZP, above),
        )

    def first(g):
        across, lift, _ = common(g)
        across().start()
        for yy in (0, 1, 2):

            @pl.when(y == yy)
            def _(yy=yy):
                for copy in table(g, yy)[None]:
                    copy().start()

        lift().start()

    def pass_on(g, role):
        arrived(g, role)
        if role == PV:
            common(g)[2]().start()
        for yy in range(4):
            if table(g, yy)[role]:

                @pl.when(y == yy)
                def _(yy=yy):
                    for copy in table(g, yy)[role]:
                        copy().start()

    order = {0: (D2O, D6O, RELAY), 1: (D6O, D2P), 2: (D6P, D2P), 3: (D6O, D2P, RELAY)}

    def later(g, which):
        for yy in range(4):
            if which < len(order[yy]):

                @pl.when(y == yy)
                def _(yy=yy):
                    role = order[yy][which]
                    arrived(g, role)
                    for copy in table(g, yy)[role]:
                        copy().start()

    def complete(g):
        for yy in range(4):

            @pl.when(y == yy)
            def _(yy=yy):
                for role in (D2O, D2P, D4O, D4P, D6O, D6P):
                    if role not in order[yy]:
                        arrived(g, role)

    def drain(g):
        for copy in common(g):
            copy().wait_send()
        for yy in range(4):

            @pl.when(y == yy)
            def _(yy=yy):
                for copies in table(g, yy).values():
                    for copy in copies:
                        copy().wait_send()

    for g in range(KEY_VALUE_HEADS):
        kvb[g, SPAN * tok : (SPAN + 1) * tok, :HEAD] = turn(kv_ref[:, g * HEAD : (g + 1) * HEAD])
        kvb[g, SPAN * tok : (SPAN + 1) * tok, HEAD:] = turn(
            kv_ref[:, (KEY_VALUE_HEADS + g) * HEAD : (KEY_VALUE_HEADS + g + 1) * HEAD]
        )

    pl.semaphore_wait(barrier, 7)
    first(0)
    first(1)

    lens[...] = jnp.zeros_like(lens)
    lens[0:1, 0:NDOC] = len_ref[...]
    lane = lax.broadcasted_iota(jnp.int32, (8, 128), 1)
    ends = lens[...]
    for step in (1, 2, 4, 8, 16, 32, 64):
        ends = ends + jnp.where(lane >= step, pltpu.roll(ends, step, 1), 0)
    starts = (ends - lens[...])[0:1, :]
    row = lax.broadcasted_iota(jnp.int32, (tok, 128), 0)
    begun = jnp.where(starts <= row + c * tok, starts, -1)
    tri[...] = jnp.broadcast_to(
        jnp.max(begun, axis=1, keepdims=True) - c * tok + SPAN * tok, (tok, 128)
    )

    q_copy.wait()
    for i in range(QUERY_HEADS):
        qr[i * tok : (i + 1) * tok, :] = turn(q_ref[:, i * HEAD : (i + 1) * HEAD])

    def score(g, slot):
        count = GROUP * tok
        q = qr[g * count : (g + 1) * count, :]
        low = tri[...]
        lanes = lax.broadcasted_iota(jnp.int32, (1, 128), 1)
        most = [jnp.full((tok, 128), LOW, jnp.float32) for _ in range(GROUP)]
        for c0 in range(0, width, CHUNK):
            n = min(CHUNK, width - c0)
            k = kvb[g, c0 : c0 + n, :HEAD]
            part = lax.dot_general(
                q, k, (((1,), (1,)), ((), ())), preferred_element_type=jnp.float32
            )
            for t in range(0, n, 128):
                place = lanes + (c0 + t)
                ok = place >= low
                if c0 + t + 127 >= SPAN * tok:
                    ok = ok & (place <= row + SPAN * tok)
                for a in range(GROUP):
                    one = jnp.where(ok, part[a * tok : (a + 1) * tok, t : t + 128], LOW)
                    scores[slot, a * tok : (a + 1) * tok, c0 + t : c0 + t + 128] = one
                    most[a] = jnp.maximum(most[a], one)
            yield
        for a in range(GROUP):
            tops[slot, a * tok : (a + 1) * tok] = jnp.broadcast_to(
                jnp.max(most[a], axis=1, keepdims=True), (tok, 128)
            )

    def mix(g, slot):
        acc = jnp.zeros((GROUP * tok, 2 * HEAD), jnp.float32)
        ones = jnp.ones((CHUNK, HEAD), jnp.bfloat16)
        top = tops[slot]
        for c0 in range(0, width, CHUNK):
            n = min(CHUNK, width - c0)
            p = jnp.concatenate(
                [
                    jnp.exp2(
                        (scores[slot, :, c0 + t : c0 + t + 128] - top) * (scale * np.log2(np.e))
                    ).astype(jnp.bfloat16)
                    for t in range(0, n, 128)
                ],
                axis=1,
            )
            v = jnp.concatenate([kvb[g, c0 : c0 + n, HEAD:], ones[:n]], axis=1)
            acc = acc + jnp.dot(p, v, preferred_element_type=jnp.float32)
            yield
        mean = acc[:, :HEAD] / acc[:, HEAD:]
        big = mean.astype(jnp.bfloat16)
        small = (mean - big.astype(jnp.float32)).astype(jnp.bfloat16)
        back = jnp.dot(big, had, preferred_element_type=jnp.float32) + jnp.dot(
            small, had, preferred_element_type=jnp.float32
        )
        back = (back * scale).astype(jnp.bfloat16)
        for a in range(GROUP):
            att[g, :, a * HEAD : (a + 1) * HEAD] = back[a * tok : (a + 1) * tok]

    def ship(g):
        return pltpu.make_async_remote_copy(
            src_ref=att.at[g],
            dst_ref=got.at[g],
            send_sem=att_send.at[g],
            recv_sem=att_recv.at[g],
            device_id=after,
            device_id_type=MESH,
        )

    last = KEY_VALUE_HEADS - 1
    pass_on(0, PV)
    pass_on(0, ZO)
    pass_on(1, PV)
    pass_on(1, ZO)
    pass_on(0, ZP)
    later(0, 0)
    first(2)
    later(0, 1)
    pass_on(1, ZP)
    pass_on(2, PV)
    pass_on(2, ZO)
    later(0, 2)
    complete(0)
    later(1, 0)
    first(3)

    def during(g):
        yield
        if g + 1 <= last:
            later(g + 1, 1)
        if g + 2 <= last:
            pass_on(g + 2, ZP)
        if g + 3 <= last:
            pass_on(g + 3, PV)
            pass_on(g + 3, ZO)
        yield
        yield
        if g + 1 <= last:
            later(g + 1, 2)
        if g + 2 <= last:
            later(g + 2, 0)

    interleave(score(0, 0), during(0))
    for g in range(1, KEY_VALUE_HEADS):
        complete(g)
        interleave(score(g, g % 2), mix(g - 1, (g - 1) % 2), during(g))
        ship(g - 1).start()
    interleave(mix(last, last % 2))
    ship(last).start()

    for g in range(KEY_VALUE_HEADS):
        drain(g)
    for g in range(KEY_VALUE_HEADS):
        ship(g).wait()

    many = QUERY_HEADS * HEAD

    def finish(i, _):
        r = pl.ds(pl.multiple_of(i * 16, 16), 16)
        x = [got[g, r, :].astype(jnp.float32) for g in range(KEY_VALUE_HEADS)]
        power = sum(jnp.sum(v * v, axis=1, keepdims=True) for v in x) / many
        factor = lax.rsqrt(power + 1e-05)
        step = GROUP * HEAD
        for g in range(KEY_VALUE_HEADS):
            out_ref[r, g * step : (g + 1) * step] = (
                x[g] * factor * gain_ref[:, g * step : (g + 1) * step]
            ).astype(jnp.bfloat16)
        return 0

    lax.fori_loop(0, tok // 16, finish, 0)


def solution(mesh):
    planes = mesh.shape["ctx"] // 8
    sections = mesh.shape["segment"]

    def body(queries, key_value_heads, doc_lengths, norm_gain):
        tok = queries.shape[1]
        width = -(-((SPAN + 1) * tok) // 128) * 128
        vmem = pl.BlockSpec(memory_space=pltpu.VMEM)
        bf16, f32 = jnp.bfloat16, jnp.float32
        out = pl.pallas_call(
            functools.partial(kernel, tok, planes, sections),
            out_shape=jax.ShapeDtypeStruct((tok, QUERY_HEADS * HEAD), bf16),
            in_specs=[pl.BlockSpec(memory_space=pl.ANY), vmem, vmem, vmem],
            out_specs=vmem,
            scratch_shapes=[
                pltpu.VMEM((tok, QUERY_HEADS * HEAD), bf16),
                pltpu.VMEM((KEY_VALUE_HEADS, SLOTS * tok, 2 * HEAD), bf16),
                pltpu.VMEM((QUERY_HEADS * tok, HEAD), bf16),
                pltpu.VMEM((2, GROUP * tok, width), f32),
                pltpu.VMEM((2, GROUP * tok, 128), f32),
                pltpu.VMEM((tok, 128), jnp.int32),
                pltpu.VMEM((KEY_VALUE_HEADS, tok, GROUP * HEAD), bf16),
                pltpu.VMEM((KEY_VALUE_HEADS, tok, GROUP * HEAD), bf16),
                pltpu.VMEM((8, 128), jnp.int32),
                pltpu.SemaphoreType.DMA,
                pltpu.SemaphoreType.DMA((KEY_VALUE_HEADS, SENDS)),
                pltpu.SemaphoreType.DMA((KEY_VALUE_HEADS, 10)),
                pltpu.SemaphoreType.DMA((KEY_VALUE_HEADS,)),
                pltpu.SemaphoreType.DMA((KEY_VALUE_HEADS,)),
            ],
            compiler_params=pltpu.CompilerParams(
                collective_id=0, has_side_effects=True, vmem_limit_bytes=62 * 2**20
            ),
        )(queries[0], key_value_heads[0], doc_lengths, norm_gain)
        return out[None]

    in_specs = (
        P("segment", "ctx", None),
        P("segment", "ctx", None),
        P("segment", None),
        P("segment", None),
    )
    return jax.shard_map(
        body, mesh=mesh, in_specs=in_specs, out_specs=P("segment", "ctx", None), check_vma=False
    )
```

```python
import functools

import jax
import jax.numpy as jnp
import numpy as np
from jax import lax
from jax.experimental import pallas as pl
from jax.experimental.pallas import tpu as pltpu
from jax.sharding import PartitionSpec as P

QUERY_HEADS = 32
KEY_VALUE_HEADS = 4
HEAD = 128
GROUP = QUERY_HEADS // KEY_VALUE_HEADS
NDOC = 64
SPAN = 8
SLOTS = SPAN + 3
MESH = pl.DeviceIdType.MESH
PV, ZO, ZP, D2O, D2P, D4O, D4P, D6O, D6P, RELAY = range(10)
SENDS = 10
CHUNK = 256
TILE = 128
HALF = GROUP // 2
LOW = -1e30


def hadamard(size):
    rows = lax.broadcasted_iota(jnp.int32, (size, size), 0)
    cols = lax.broadcasted_iota(jnp.int32, (size, size), 1)
    both = rows & cols
    both = both ^ (both >> 4)
    both = both ^ (both >> 2)
    both = both ^ (both >> 1)
    return jnp.where((both & 1) == 0, 1.0, -1.0).astype(jnp.bfloat16)


def kernel(
    tok, planes, sections,
    q_hbm, kv_ref, len_ref, got,
    q_ref, kvb, qr, scores, sums, tops, fade, tri, att, lens,
    q_sem, send_sem, recv_sem, att_send, att_recv,
):
    width = -(-((SPAN + 1) * tok) // 128) * 128
    scale = HEAD ** (-0.5)
    c = lax.axis_index("ctx")
    s = lax.axis_index("segment")
    h = lax.rem(c, 2)
    y = lax.rem(c // 2, 4)
    z = c // 8
    e = 1 - 2 * h
    up = lax.rem(z + 1, planes)
    down = lax.rem(z + planes - 1, planes)
    right = lax.rem(y + 1, 4)
    left = lax.rem(y + 3, 4)

    def at(zz, yy, hh):
        return zz * 8 + yy * 2 + hh

    partner = {"ctx": at(z, y, 1 - h)}
    above = {"ctx": at(up, y, h)}
    below = {"ctx": at(down, y, h)}
    to_right = {"ctx": at(z, right, h)}
    to_left = {"ctx": at(z, left, h)}
    after = {"segment": lax.rem(s + 1, sections)}
    before = {"segment": lax.rem(s + sections - 1, sections)}

    q_copy = pltpu.make_async_copy(q_hbm, q_ref, q_sem)
    q_copy.start()
    barrier = pltpu.get_barrier_semaphore()
    for who in (partner, below, above, to_right, to_left, before, after):
        pl.semaphore_signal(barrier, inc=1, device_id=who, device_id_type=MESH)

    had = hadamard(HEAD)

    def turn(x):
        return (jnp.dot(x, had, preferred_element_type=jnp.float32) * scale).astype(jnp.bfloat16)

    def rows(slot):
        return pl.ds(pl.multiple_of(slot * tok, 16), tok)

    def send(g, k, src, dst, role, who):
        return pltpu.make_async_remote_copy(
            src_ref=kvb.at[g, rows(src), :],
            dst_ref=kvb.at[g, rows(dst), :],
            send_sem=send_sem.at[g, k],
            recv_sem=recv_sem.at[g, role],
            device_id=who,
            device_id_type=MESH,
        )

    def arrived(g, role):
        pltpu.make_async_remote_copy(
            src_ref=kvb.at[g, rows(0), :],
            dst_ref=kvb.at[g, rows(0), :],
            send_sem=send_sem.at[g, 0],
            recv_sem=recv_sem.at[g, role],
            device_id=partner,
            device_id_type=MESH,
        ).wait_recv()

    pv = SPAN + e
    pp = lax.rem(e + 10, 10)

    def table(g, yy):
        entries = {None: [], PV: [], ZO: [], ZP: [], D2O: [], D2P: [], D6O: [], D6P: [], RELAY: []}
        count = [3]

        def add(when, src, dst, role, who):
            entries[when].append(functools.partial(send, g, count[0], src, dst, role, who))
            count[0] += 1

        v_dirs = {0: (1, 3), 1: (1,), 2: (1,), 3: ()}[yy]
        p_dirs = {0: (), 1: (-1,), 2: (-1,), 3: (-3, -1)}[yy]
        for d in v_dirs:
            who = to_right if d == 1 else to_left
            own, pair = (D6O, D6P) if d == 1 else (D2O, D2P)
            add(None, SPAN, SPAN - 2 * d, own, who)
            add(PV, pv, SPAN - 2 * d + e, pair, who)
        for d in p_dirs:
            who = to_right if d == -3 else to_left
            own, pair = (D6O, D6P) if d == -3 else (D2O, D2P)
            add(ZO, 0, -2 * d, own, who)
            add(ZP, pp, -2 * d + e, pair, who)
        if yy == 0:
            add(D6O, 6, 4, D4O, to_right)
            add(D2O, 2, 10, RELAY, below)
            add(RELAY, 10, 4, D4O, to_left)
        if yy == 1:
            add(D6O, 6, 4, D4O, to_right)
            add(D2P, 2 + e, 4 + e, D4P, to_left)
        if yy == 2:
            add(D6P, 6 + e, 4 + e, D4P, to_right)
            add(D2P, 2 + e, 4 + e, D4P, to_left)
        if yy == 3:
            add(D2P, 2 + e, 4 + e, D4P, to_left)
            add(D6O, 6, 10, RELAY, above)
            add(RELAY, 10, 4, D4O, to_right)
        return entries

    def common(g):
        return (
            functools.partial(send, g, 0, SPAN, SPAN - e, PV, partner),
            functools.partial(send, g, 1, SPAN, 0, ZO, above),
            functools.partial(send, g, 2, pv, pp, ZP, above),
        )

    def only(places, run):
        for yy in places:
            pl.when(y == yy)(functools.partial(run, yy))

    def across(g):
        common(g)[0]().start()

    def own(g):
        def run(yy):
            for copy in table(g, yy)[None]:
                copy().start()

        only((0, 1, 2), run)
        common(g)[1]().start()

    def pass_on(g, role, places=(0, 1, 2, 3)):
        def run(yy):
            for copy in table(g, yy)[role]:
                copy().start()

        arrived(g, role)
        if role == PV:
            common(g)[2]().start()
        only([yy for yy in places if table(g, yy)[role]], run)

    own_roles = {0: (D2O, D6O), 1: (D6O,), 3: (D6O,)}
    near_roles = {1: (D6O,), 3: (D6O,)}
    far_roles = {0: (D2O, D6O)}
    pair_roles = {1: (D2P,), 2: (D6P, D2P), 3: (D2P,)}
    relay_roles = {0: (RELAY,), 3: (RELAY,)}

    def onward(g, roles):
        def run(yy):
            for role in roles[yy]:
                arrived(g, role)
                for copy in table(g, yy)[role]:
                    copy().start()

        only(roles, run)

    def complete(g):
        def run(yy):
            seen = own_roles.get(yy, ()) + pair_roles.get(yy, ())
            for role in (D2O, D2P, D6O, D6P):
                if role not in seen:
                    arrived(g, role)

        only(range(4), run)

    def complete_last(g):
        arrived(g, D4O)
        arrived(g, D4P)

    def drain(g):
        for copy in common(g):
            copy().wait_send()
        for yy in range(4):

            @pl.when(y == yy)
            def _(yy=yy):
                for copies in table(g, yy).values():
                    for copy in copies:
                        copy().wait_send()

    def block(run, *args):
        pl.when(c >= 0)(functools.partial(run, *args))

    def rotate(g):
        kvb[g, SPAN * tok : (SPAN + 1) * tok, :HEAD] = turn(kv_ref[:, g * HEAD : (g + 1) * HEAD])
        kvb[g, SPAN * tok : (SPAN + 1) * tok, HEAD:] = turn(
            kv_ref[:, (KEY_VALUE_HEADS + g) * HEAD : (KEY_VALUE_HEADS + g + 1) * HEAD]
        )

    block(rotate, 0)
    block(rotate, 1)
    pl.semaphore_wait(barrier, 7)
    for g in (0, 1):
        across(g)
        own(g)
    block(rotate, 2)
    block(rotate, 3)
    across(2)
    across(3)

    lens[...] = jnp.zeros_like(lens)
    lens[0:1, 0:NDOC] = len_ref[...]
    lane = lax.broadcasted_iota(jnp.int32, (8, 128), 1)
    ends = lens[...]
    for step in (1, 2, 4, 8, 16, 32, 64):
        ends = ends + jnp.where(lane >= step, pltpu.roll(ends, step, 1), 0)
    starts = (ends - lens[...])[0:1, :]
    row = lax.broadcasted_iota(jnp.int32, (tok, 128), 0)
    begun = jnp.where(starts <= row + c * tok, starts, -1)
    tri[...] = jnp.broadcast_to(
        jnp.max(begun, axis=1, keepdims=True) - c * tok + SPAN * tok, (tok, 128)
    )

    q_copy.wait()

    def rotate_queries(i):
        for a in range(i * GROUP, (i + 1) * GROUP):
            qr[a * tok : (a + 1) * tok, :] = turn(q_ref[:, a * HEAD : (a + 1) * HEAD])

    tiles = width // TILE
    late = list(range((SPAN // 2 - 1) * tok // TILE, -(-(SPAN // 2 + 2) * tok // TILE)))
    before_late, after_late = list(range(late[0])), list(range(late[-1] + 1, tiles))

    def paired(some):
        return [some[i : i + 2] for i in range(0, len(some), 2)]

    early_pairs = paired(before_late) + paired(after_late)
    late_pairs = paired(late)
    factor = scale * np.log2(np.e)

    def score(g, pairs):
        count = GROUP * tok
        q = qr[g * count : (g + 1) * count, :]
        low = tri[...]
        lanes = lax.broadcasted_iota(jnp.int32, (1, TILE), 1)
        most = [jnp.full((tok, TILE), LOW, jnp.float32) for _ in range(GROUP)]
        for n, t in enumerate(sum(pairs, [])):
            k = kvb[g, t * TILE : (t + 1) * TILE, :HEAD]
            part = lax.dot_general(
                q, k, (((1,), (1,)), ((), ())), preferred_element_type=jnp.float32
            )
            place = lanes + t * TILE
            ok = place >= low
            if (t + 1) * TILE > SPAN * tok:
                ok = ok & (place <= row + SPAN * tok)
            for a in range(GROUP):
                one = jnp.where(ok, part[a * tok : (a + 1) * tok], LOW)
                scores[a * tok : (a + 1) * tok, n * TILE : (n + 1) * TILE] = one
                most[a] = jnp.maximum(most[a], one)
        return [
            jnp.broadcast_to(jnp.max(top, axis=1, keepdims=True), (tok, TILE)) for top in most
        ]

    def score_early(g):
        for a, top in enumerate(score(g, early_pairs)):
            tops[g, a * tok : (a + 1) * tok] = top

    def score_late(g):
        for a, top in enumerate(score(g, late_pairs)):
            r = slice(a * tok, (a + 1) * tok)
            old = tops[g, r]
            top = jnp.maximum(old, top)
            fade[r] = jnp.exp2((old - top) * factor)
            tops[g, r] = top

    def weigh(g, span, acc, pairs):
        ones = jnp.ones((2 * TILE, HEAD), jnp.bfloat16)
        top = tops[g, span]
        n = 0
        for pair in pairs:
            p = []
            for _ in pair:
                part = scores[span, n * TILE : (n + 1) * TILE]
                p.append(jnp.exp2((part - top) * factor).astype(jnp.bfloat16))
                n += 1
            keys = len(pair) * TILE
            v = kvb[g, pair[0] * TILE : pair[0] * TILE + keys, HEAD:]
            v = jnp.concatenate([v, ones[:keys]], axis=1)
            p = jnp.concatenate(p, axis=1)
            acc = acc + jnp.dot(p, v, preferred_element_type=jnp.float32)
        return acc

    def mix_early(g, half):
        span = slice(half * HALF * tok, (half + 1) * HALF * tok)
        zero = jnp.zeros((HALF * tok, 2 * HEAD), jnp.float32)
        sums[g, span] = weigh(g, span, zero, early_pairs)

    def mix_late(g, half):
        span = slice(half * HALF * tok, (half + 1) * HALF * tok)
        old = fade[span]
        acc = sums[g, span] * jnp.concatenate([old, old], axis=1)
        acc = weigh(g, span, acc, late_pairs)
        mean = acc[:, :HEAD] / acc[:, HEAD:]
        big = mean.astype(jnp.bfloat16)
        small = (mean - big.astype(jnp.float32)).astype(jnp.bfloat16)
        back = jnp.dot(big, had, preferred_element_type=jnp.float32) + jnp.dot(
            small, had, preferred_element_type=jnp.float32
        )
        back = (back * scale).astype(jnp.bfloat16)
        for a in range(HALF):
            att[2 * g + half, :, a * HEAD : (a + 1) * HEAD] = back[a * tok : (a + 1) * tok]

    def ship(i):
        return pltpu.make_async_remote_copy(
            src_ref=att.at[i],
            dst_ref=got.at[i],
            send_sem=att_send.at[i],
            recv_sem=att_recv.at[i],
            device_id=after,
            device_id_type=MESH,
        )

    def early_score(g):
        complete(g)
        block(score_early, g)

    def early_mix(g, half):
        block(mix_early, g, half)

    def late_score(g):
        complete_last(g)
        block(score_late, g)

    def late_mix(g, half):
        block(mix_late, g, half)
        ship(2 * g + half).start()

    def turn_queries(i):
        block(rotate_queries, i)

    def near(g):
        onward(g, near_roles)

    def far(g):
        onward(g, far_roles)

    def pairs_on(g):
        onward(g, pair_roles)

    def relays(g):
        onward(g, relay_roles)

    for step in (
        (turn_queries, 0), (pass_on, 0, ZO), (pass_on, 0, PV), (near, 0), (own, 2),
        (turn_queries, 1), (pass_on, 1, ZO), (pass_on, 1, PV), (near, 1), (own, 3),
        (turn_queries, 2), (far, 0), (pass_on, 0, ZP), (pass_on, 2, PV), (near, 2),
        (turn_queries, 3), (pass_on, 2, ZO), (far, 1), (relays, 0), (pairs_on, 0),
        (pass_on, 1, ZP), (pass_on, 3, PV), (near, 3),
        (early_score, 0), (pass_on, 3, ZO), (far, 2), (early_mix, 0, 0), (relays, 1),
        (early_mix, 0, 1), (pairs_on, 1), (pass_on, 2, ZP),
        (early_score, 1), (early_mix, 1, 0), (far, 3), (relays, 2), (early_mix, 1, 1),
        (late_score, 0), (late_mix, 0, 0), (pairs_on, 2), (pass_on, 3, ZP), (late_mix, 0, 1),
        (early_score, 2), (early_mix, 2, 0), (relays, 3), (early_mix, 2, 1),
        (late_score, 1), (late_mix, 1, 0), (pairs_on, 3), (late_mix, 1, 1),
        (early_score, 3), (early_mix, 3, 0), (early_mix, 3, 1),
        (late_score, 2), (late_mix, 2, 0), (late_mix, 2, 1),
        (late_score, 3), (late_mix, 3, 0), (late_mix, 3, 1),
    ):
        step[0](*step[1:])

    for g in range(KEY_VALUE_HEADS):
        drain(g)
    for i in range(2 * KEY_VALUE_HEADS):
        ship(i).wait()


def finish(got_ref, gain_ref, out_ref):
    parts, _, step = got_ref.shape
    x = [got_ref[i].astype(jnp.float32) for i in range(parts)]
    power = sum(jnp.sum(v * v, axis=1, keepdims=True) for v in x) / (parts * step)
    factor = lax.rsqrt(power + 1e-05)
    for i in range(parts):
        out_ref[:, i * step : (i + 1) * step] = (
            x[i] * factor * gain_ref[:, i * step : (i + 1) * step]
        ).astype(jnp.bfloat16)


def solution(mesh):
    planes = mesh.shape["ctx"] // 8
    sections = mesh.shape["segment"]

    def body(queries, key_value_heads, doc_lengths, norm_gain):
        tok = queries.shape[1]
        width = -(-((SPAN + 1) * tok) // 128) * 128
        vmem = pl.BlockSpec(memory_space=pltpu.VMEM)
        bf16, f32 = jnp.bfloat16, jnp.float32
        parts, step = 2 * KEY_VALUE_HEADS, HALF * HEAD
        got = pl.pallas_call(
            functools.partial(kernel, tok, planes, sections),
            out_shape=jax.ShapeDtypeStruct((parts, tok, step), bf16),
            in_specs=[pl.BlockSpec(memory_space=pl.ANY), vmem, vmem],
            out_specs=pl.BlockSpec(memory_space=pl.ANY),
            scratch_shapes=[
                pltpu.VMEM((tok, QUERY_HEADS * HEAD), bf16),
                pltpu.VMEM((KEY_VALUE_HEADS, SLOTS * tok, 2 * HEAD), bf16),
                pltpu.VMEM((QUERY_HEADS * tok, HEAD), bf16),
                pltpu.VMEM((GROUP * tok, width), f32),
                pltpu.VMEM((KEY_VALUE_HEADS, GROUP * tok, 2 * HEAD), f32),
                pltpu.VMEM((KEY_VALUE_HEADS, GROUP * tok, TILE), f32),
                pltpu.VMEM((GROUP * tok, TILE), f32),
                pltpu.VMEM((tok, TILE), jnp.int32),
                pltpu.VMEM((parts, tok, step), bf16),
                pltpu.VMEM((8, 128), jnp.int32),
                pltpu.SemaphoreType.DMA,
                pltpu.SemaphoreType.DMA((KEY_VALUE_HEADS, SENDS)),
                pltpu.SemaphoreType.DMA((KEY_VALUE_HEADS, 10)),
                pltpu.SemaphoreType.DMA((parts,)),
                pltpu.SemaphoreType.DMA((parts,)),
            ],
            compiler_params=pltpu.CompilerParams(
                collective_id=0, has_side_effects=True, vmem_limit_bytes=60 * 2**20
            ),
        )(queries[0], key_value_heads[0], doc_lengths)
        rows = tok // 2 if tok % 16 == 0 else tok
        out = pl.pallas_call(
            finish,
            grid=(tok // rows,),
            out_shape=jax.ShapeDtypeStruct((tok, QUERY_HEADS * HEAD), bf16),
            in_specs=[
                pl.BlockSpec((parts, rows, step), lambda i: (0, i, 0)),
                pl.BlockSpec((1, QUERY_HEADS * HEAD), lambda i: (0, 0)),
            ],
            out_specs=pl.BlockSpec((rows, QUERY_HEADS * HEAD), lambda i: (i, 0)),
        )(got, norm_gain)
        return out[None]

    in_specs = (
        P("segment", "ctx", None),
        P("segment", "ctx", None),
        P("segment", None),
        P("segment", None),
    )
    return jax.shard_map(
        body, mesh=mesh, in_specs=in_specs, out_specs=P("segment", "ctx", None), check_vma=False
    )
```

```python
import functools

import jax
import jax.numpy as jnp
import numpy as np
from jax import lax
from jax.experimental import pallas as pl
from jax.experimental.pallas import tpu as pltpu
from jax.sharding import PartitionSpec as P

QUERY_HEADS = 32
KEY_VALUE_HEADS = 4
HEAD = 128
GROUP = QUERY_HEADS // KEY_VALUE_HEADS
NDOC = 64
SPAN = 8
SLOTS = SPAN + 3
MESH = pl.DeviceIdType.MESH
PV, ZO, ZP, D2O, D2P, D4O, D4P, D6O, D6P, RELAY = range(10)
SENDS = 10
CHUNK = 256
TILE = 128
HALF = GROUP // 2
LOW = -1e30


def hadamard(size):
    rows = lax.broadcasted_iota(jnp.int32, (size, size), 0)
    cols = lax.broadcasted_iota(jnp.int32, (size, size), 1)
    both = rows & cols
    both = both ^ (both >> 4)
    both = both ^ (both >> 2)
    both = both ^ (both >> 1)
    return jnp.where((both & 1) == 0, 1.0, -1.0).astype(jnp.bfloat16)


def kernel(
    tok, planes, sections,
    q_hbm, kv_hbm, len_ref, got,
    q_ref, kv_ref, kvb, qr, scores, sums, tops, fade, tri, att, lens,
    q_sem, kv_sem, send_sem, recv_sem, att_send, att_recv,
):
    width = -(-((SPAN + 1) * tok) // 128) * 128
    scale = HEAD ** (-0.5)
    c = lax.axis_index("ctx")
    s = lax.axis_index("segment")
    h = lax.rem(c, 2)
    y = lax.rem(c // 2, 4)
    z = c // 8
    e = 1 - 2 * h
    up = lax.rem(z + 1, planes)
    down = lax.rem(z + planes - 1, planes)
    right = lax.rem(y + 1, 4)
    left = lax.rem(y + 3, 4)

    def at(zz, yy, hh):
        return zz * 8 + yy * 2 + hh

    partner = {"ctx": at(z, y, 1 - h)}
    above = {"ctx": at(up, y, h)}
    below = {"ctx": at(down, y, h)}
    to_right = {"ctx": at(z, right, h)}
    to_left = {"ctx": at(z, left, h)}
    after = {"segment": lax.rem(s + 1, sections)}
    before = {"segment": lax.rem(s + sections - 1, sections)}

    kv_copy = pltpu.make_async_copy(kv_hbm, kv_ref, kv_sem)
    kv_copy.start()
    q_copy = pltpu.make_async_copy(q_hbm, q_ref, q_sem)
    q_copy.start()
    barrier = pltpu.get_barrier_semaphore()
    for who in (partner, below, above, to_right, to_left, before, after):
        pl.semaphore_signal(barrier, inc=1, device_id=who, device_id_type=MESH)

    had = hadamard(HEAD)

    def turn(x):
        return (jnp.dot(x, had, preferred_element_type=jnp.float32) * scale).astype(jnp.bfloat16)

    def rows(slot):
        return pl.ds(pl.multiple_of(slot * tok, 16), tok)

    def send(g, k, src, dst, role, who):
        return pltpu.make_async_remote_copy(
            src_ref=kvb.at[g, rows(src), :],
            dst_ref=kvb.at[g, rows(dst), :],
            send_sem=send_sem.at[g, k],
            recv_sem=recv_sem.at[g, role],
            device_id=who,
            device_id_type=MESH,
        )

    def arrived(g, role):
        pltpu.make_async_remote_copy(
            src_ref=kvb.at[g, rows(0), :],
            dst_ref=kvb.at[g, rows(0), :],
            send_sem=send_sem.at[g, 0],
            recv_sem=recv_sem.at[g, role],
            device_id=partner,
            device_id_type=MESH,
        ).wait_recv()

    pv = SPAN + e
    pp = lax.rem(e + 10, 10)

    def table(g, yy):
        entries = {None: [], PV: [], ZO: [], ZP: [], D2O: [], D2P: [], D6O: [], D6P: [], RELAY: []}
        count = [3]

        def add(when, src, dst, role, who):
            entries[when].append(functools.partial(send, g, count[0], src, dst, role, who))
            count[0] += 1

        v_dirs = {0: (1, 3), 1: (1,), 2: (1,), 3: ()}[yy]
        p_dirs = {0: (), 1: (-1,), 2: (-1,), 3: (-3, -1)}[yy]
        for d in v_dirs:
            who = to_right if d == 1 else to_left
            own, pair = (D6O, D6P) if d == 1 else (D2O, D2P)
            add(None, SPAN, SPAN - 2 * d, own, who)
            add(PV, pv, SPAN - 2 * d + e, pair, who)
        for d in p_dirs:
            who = to_right if d == -3 else to_left
            own, pair = (D6O, D6P) if d == -3 else (D2O, D2P)
            add(ZO, 0, -2 * d, own, who)
            add(ZP, pp, -2 * d + e, pair, who)
        if yy == 0:
            add(D6O, 6, 4, D4O, to_right)
            add(D2O, 2, 10, RELAY, below)
            add(RELAY, 10, 4, D4O, to_left)
        if yy == 1:
            add(D6O, 6, 4, D4O, to_right)
            add(D2P, 2 + e, 4 + e, D4P, to_left)
        if yy == 2:
            add(D6P, 6 + e, 4 + e, D4P, to_right)
            add(D2P, 2 + e, 4 + e, D4P, to_left)
        if yy == 3:
            add(D2P, 2 + e, 4 + e, D4P, to_left)
            add(D6O, 6, 10, RELAY, above)
            add(RELAY, 10, 4, D4O, to_right)
        return entries

    def common(g):
        return (
            functools.partial(send, g, 0, SPAN, SPAN - e, PV, partner),
            functools.partial(send, g, 1, SPAN, 0, ZO, above),
            functools.partial(send, g, 2, pv, pp, ZP, above),
        )

    def only(places, run):
        for yy in places:
            pl.when(y == yy)(functools.partial(run, yy))

    def across(g):
        common(g)[0]().start()

    def own(g):
        def run(yy):
            for copy in table(g, yy)[None]:
                copy().start()

        only((0, 1, 2), run)
        common(g)[1]().start()

    def pass_on(g, role, places=(0, 1, 2, 3)):
        def run(yy):
            for copy in table(g, yy)[role]:
                copy().start()

        arrived(g, role)
        if role == PV:
            common(g)[2]().start()
        only([yy for yy in places if table(g, yy)[role]], run)

    own_roles = {0: (D2O, D6O), 1: (D6O,), 3: (D6O,)}
    near_roles = {1: (D6O,), 3: (D6O,)}
    far_roles = {0: (D2O, D6O)}
    pair_roles = {1: (D2P,), 2: (D6P, D2P), 3: (D2P,)}
    relay_roles = {0: (RELAY,), 3: (RELAY,)}

    def onward(g, roles):
        def run(yy):
            for role in roles[yy]:
                arrived(g, role)
                for copy in table(g, yy)[role]:
                    copy().start()

        only(roles, run)

    def complete(g):
        def run(yy):
            seen = own_roles.get(yy, ()) + pair_roles.get(yy, ())
            for role in (D2O, D2P, D6O, D6P):
                if role not in seen:
                    arrived(g, role)

        only(range(4), run)

    def complete_last(g):
        arrived(g, D4O)
        arrived(g, D4P)

    def drain(g):
        for copy in common(g):
            copy().wait_send()
        for yy in range(4):

            @pl.when(y == yy)
            def _(yy=yy):
                for copies in table(g, yy).values():
                    for copy in copies:
                        copy().wait_send()

    def block(run, *args):
        pl.when(c >= 0)(functools.partial(run, *args))

    def rotate(g):
        kvb[g, SPAN * tok : (SPAN + 1) * tok, :HEAD] = turn(kv_ref[:, g * HEAD : (g + 1) * HEAD])
        kvb[g, SPAN * tok : (SPAN + 1) * tok, HEAD:] = turn(
            kv_ref[:, (KEY_VALUE_HEADS + g) * HEAD : (KEY_VALUE_HEADS + g + 1) * HEAD]
        )

    kv_copy.wait()
    block(rotate, 0)
    block(rotate, 1)
    pl.semaphore_wait(barrier, 7)
    for g in (0, 1):
        across(g)
        own(g)
    block(rotate, 2)
    block(rotate, 3)
    across(2)
    across(3)

    lens[...] = jnp.zeros_like(lens)
    lens[0:1, 0:NDOC] = len_ref[...]
    lane = lax.broadcasted_iota(jnp.int32, (8, 128), 1)
    ends = lens[...]
    for step in (1, 2, 4, 8, 16, 32, 64):
        ends = ends + jnp.where(lane >= step, pltpu.roll(ends, step, 1), 0)
    starts = (ends - lens[...])[0:1, :]
    row = lax.broadcasted_iota(jnp.int32, (tok, 128), 0)
    begun = jnp.where(starts <= row + c * tok, starts, -1)
    tri[...] = jnp.broadcast_to(
        jnp.max(begun, axis=1, keepdims=True) - c * tok + SPAN * tok, (tok, 128)
    )

    q_copy.wait()

    def rotate_queries(i):
        for a in range(i * GROUP, (i + 1) * GROUP):
            qr[a * tok : (a + 1) * tok, :] = turn(q_ref[:, a * HEAD : (a + 1) * HEAD])

    tiles = width // TILE
    late = list(range((SPAN // 2 - 1) * tok // TILE, -(-(SPAN // 2 + 2) * tok // TILE)))
    before_late, after_late = list(range(late[0])), list(range(late[-1] + 1, tiles))

    def paired(some):
        return [some[i : i + 2] for i in range(0, len(some), 2)]

    early_pairs = paired(before_late) + paired(after_late)
    late_pairs = paired(late)
    factor = scale * np.log2(np.e)

    def score(g, pairs):
        count = GROUP * tok
        q = qr[g * count : (g + 1) * count, :]
        low = tri[...]
        lanes = lax.broadcasted_iota(jnp.int32, (1, TILE), 1)
        most = [jnp.full((tok, TILE), LOW, jnp.float32) for _ in range(GROUP)]
        for n, t in enumerate(sum(pairs, [])):
            k = kvb[g, t * TILE : (t + 1) * TILE, :HEAD]
            part = lax.dot_general(
                q, k, (((1,), (1,)), ((), ())), preferred_element_type=jnp.float32
            )
            place = lanes + t * TILE
            ok = place >= low
            if (t + 1) * TILE > SPAN * tok:
                ok = ok & (place <= row + SPAN * tok)
            for a in range(GROUP):
                one = jnp.where(ok, part[a * tok : (a + 1) * tok], LOW)
                scores[a * tok : (a + 1) * tok, n * TILE : (n + 1) * TILE] = one
                most[a] = jnp.maximum(most[a], one)
        return [
            jnp.broadcast_to(jnp.max(top, axis=1, keepdims=True), (tok, TILE)) for top in most
        ]

    def score_early(g):
        for a, top in enumerate(score(g, early_pairs)):
            tops[g, a * tok : (a + 1) * tok] = top

    def score_late(g):
        for a, top in enumerate(score(g, late_pairs)):
            r = slice(a * tok, (a + 1) * tok)
            old = tops[g, r]
            top = jnp.maximum(old, top)
            fade[r] = jnp.exp2((old - top) * factor)
            tops[g, r] = top

    def weigh(g, span, acc, pairs):
        ones = jnp.ones((2 * TILE, HEAD), jnp.bfloat16)
        top = tops[g, span]
        n = 0
        for pair in pairs:
            p = []
            for _ in pair:
                part = scores[span, n * TILE : (n + 1) * TILE]
                p.append(jnp.exp2((part - top) * factor).astype(jnp.bfloat16))
                n += 1
            keys = len(pair) * TILE
            v = kvb[g, pair[0] * TILE : pair[0] * TILE + keys, HEAD:]
            v = jnp.concatenate([v, ones[:keys]], axis=1)
            p = jnp.concatenate(p, axis=1)
            acc = acc + jnp.dot(p, v, preferred_element_type=jnp.float32)
        return acc

    def mix_early(g, half):
        span = slice(half * HALF * tok, (half + 1) * HALF * tok)
        zero = jnp.zeros((HALF * tok, 2 * HEAD), jnp.float32)
        sums[g, span] = weigh(g, span, zero, early_pairs)

    def mix_late(g, half):
        span = slice(half * HALF * tok, (half + 1) * HALF * tok)
        old = fade[span]
        acc = sums[g, span] * jnp.concatenate([old, old], axis=1)
        acc = weigh(g, span, acc, late_pairs)
        mean = acc[:, :HEAD] / acc[:, HEAD:]
        big = mean.astype(jnp.bfloat16)
        small = (mean - big.astype(jnp.float32)).astype(jnp.bfloat16)
        back = jnp.dot(big, had, preferred_element_type=jnp.float32) + jnp.dot(
            small, had, preferred_element_type=jnp.float32
        )
        back = (back * scale).astype(jnp.bfloat16)
        for a in range(HALF):
            att[2 * g + half, :, a * HEAD : (a + 1) * HEAD] = back[a * tok : (a + 1) * tok]

    def ship(i):
        return pltpu.make_async_remote_copy(
            src_ref=att.at[i],
            dst_ref=got.at[i],
            send_sem=att_send.at[i],
            recv_sem=att_recv.at[i],
            device_id=after,
            device_id_type=MESH,
        )

    def early_score(g):
        complete(g)
        block(score_early, g)

    def early_mix(g, half):
        block(mix_early, g, half)

    def late_score(g):
        complete_last(g)
        block(score_late, g)

    def late_mix(g, half):
        block(mix_late, g, half)
        ship(2 * g + half).start()

    def turn_queries(i):
        block(rotate_queries, i)

    def near(g):
        onward(g, near_roles)

    def far(g):
        onward(g, far_roles)

    def pairs_on(g):
        onward(g, pair_roles)

    def relays(g):
        onward(g, relay_roles)

    for step in (
        (turn_queries, 0), (pass_on, 0, ZO), (pass_on, 0, PV), (near, 0), (own, 2),
        (turn_queries, 1), (pass_on, 1, ZO), (pass_on, 1, PV), (near, 1), (own, 3),
        (turn_queries, 2), (far, 0), (pass_on, 0, ZP), (pass_on, 2, PV), (near, 2),
        (turn_queries, 3), (pass_on, 2, ZO), (far, 1), (relays, 0), (pairs_on, 0),
        (pass_on, 1, ZP), (pass_on, 3, PV), (near, 3),
        (early_score, 0), (pass_on, 3, ZO), (early_mix, 0, 0), (far, 2), (relays, 1),
        (early_mix, 0, 1), (pairs_on, 1), (pass_on, 2, ZP),
        (early_score, 1), (early_mix, 1, 0), (relays, 2), (early_mix, 1, 1),
        (late_score, 0), (late_mix, 0, 0), (far, 3), (pairs_on, 2), (pass_on, 3, ZP), (late_mix, 0, 1),
        (early_score, 2), (early_mix, 2, 0), (early_mix, 2, 1),
        (late_score, 1), (late_mix, 1, 0), (relays, 3), (pairs_on, 3), (late_mix, 1, 1),
        (early_score, 3), (early_mix, 3, 0), (early_mix, 3, 1),
        (late_score, 2), (late_mix, 2, 0), (late_mix, 2, 1),
        (late_score, 3), (late_mix, 3, 0), (late_mix, 3, 1),
    ):
        step[0](*step[1:])

    for g in range(KEY_VALUE_HEADS):
        drain(g)
    for i in range(2 * KEY_VALUE_HEADS):
        ship(i).wait()


def finish(got_ref, gain_ref, out_ref):
    parts, _, step = got_ref.shape
    x = [got_ref[i].astype(jnp.float32) for i in range(parts)]
    power = sum(jnp.sum(v * v, axis=1, keepdims=True) for v in x) / (parts * step)
    factor = lax.rsqrt(power + 1e-05)
    for i in range(parts):
        out_ref[:, i * step : (i + 1) * step] = (
            x[i] * factor * gain_ref[:, i * step : (i + 1) * step]
        ).astype(jnp.bfloat16)


def solution(mesh):
    planes = mesh.shape["ctx"] // 8
    sections = mesh.shape["segment"]

    def body(queries, key_value_heads, doc_lengths, norm_gain):
        tok = queries.shape[1]
        width = -(-((SPAN + 1) * tok) // 128) * 128
        vmem = pl.BlockSpec(memory_space=pltpu.VMEM)
        bf16, f32 = jnp.bfloat16, jnp.float32
        parts, step = 2 * KEY_VALUE_HEADS, HALF * HEAD
        got = pl.pallas_call(
            functools.partial(kernel, tok, planes, sections),
            out_shape=jax.ShapeDtypeStruct((parts, tok, step), bf16),
            in_specs=[pl.BlockSpec(memory_space=pl.ANY), pl.BlockSpec(memory_space=pl.ANY), vmem],
            out_specs=pl.BlockSpec(memory_space=pl.ANY),
            scratch_shapes=[
                pltpu.VMEM((tok, QUERY_HEADS * HEAD), bf16),
                pltpu.VMEM((tok, 2 * KEY_VALUE_HEADS * HEAD), bf16),
                pltpu.VMEM((KEY_VALUE_HEADS, SLOTS * tok, 2 * HEAD), bf16),
                pltpu.VMEM((QUERY_HEADS * tok, HEAD), bf16),
                pltpu.VMEM((GROUP * tok, width), f32),
                pltpu.VMEM((KEY_VALUE_HEADS, GROUP * tok, 2 * HEAD), f32),
                pltpu.VMEM((KEY_VALUE_HEADS, GROUP * tok, TILE), f32),
                pltpu.VMEM((GROUP * tok, TILE), f32),
                pltpu.VMEM((tok, TILE), jnp.int32),
                pltpu.VMEM((parts, tok, step), bf16),
                pltpu.VMEM((8, 128), jnp.int32),
                pltpu.SemaphoreType.DMA,
                pltpu.SemaphoreType.DMA,
                pltpu.SemaphoreType.DMA((KEY_VALUE_HEADS, SENDS)),
                pltpu.SemaphoreType.DMA((KEY_VALUE_HEADS, 10)),
                pltpu.SemaphoreType.DMA((parts,)),
                pltpu.SemaphoreType.DMA((parts,)),
            ],
            compiler_params=pltpu.CompilerParams(
                collective_id=0, has_side_effects=True, vmem_limit_bytes=60 * 2**20
            ),
        )(queries[0], key_value_heads[0], doc_lengths)
        rows = tok // 2 if tok % 16 == 0 else tok
        out = pl.pallas_call(
            finish,
            grid=(tok // rows,),
            out_shape=jax.ShapeDtypeStruct((tok, QUERY_HEADS * HEAD), bf16),
            in_specs=[
                pl.BlockSpec((parts, rows, step), lambda i: (0, i, 0)),
                pl.BlockSpec((1, QUERY_HEADS * HEAD), lambda i: (0, 0)),
            ],
            out_specs=pl.BlockSpec((rows, QUERY_HEADS * HEAD), lambda i: (i, 0)),
        )(got, norm_gain)
        return out[None]

    in_specs = (
        P("segment", "ctx", None),
        P("segment", "ctx", None),
        P("segment", None),
        P("segment", None),
    )
    return jax.shard_map(
        body, mesh=mesh, in_specs=in_specs, out_specs=P("segment", "ctx", None), check_vma=False
    )
```
